256 devices in a mesh: mem: 16 (over x_hi, y, core), tile: 16 (over x_lo, z).
Axes of the slice: x: 4 (x_hi: 2, x_lo: 2; x = x_hi * 2 + x_lo), y: 4, z: 8, core: 2. Of those that a mesh axis runs over, the one named last changes fastest.
Arguments:
- alpha: bfloat16 [16, 16, 720, 1440], P('mem', None, 'tile'), may hold values from -6 to 6
- perturbation: bfloat16 [16, 16, 720, 1440], P('mem', None, 'tile'), may hold values from -3 to 3
- lon_scale: float32 [16], replicated, may hold values from 8 to 48
- lat_scale: float32 [16], replicated, may hold values from 12 to 64
- obs_level: int32 [16, 16384], P('tile'), may hold values from 0 to 15
- obs_row: int32 [16, 16384], P('tile'), may hold values from 0 to 44
- obs_col: int32 [16, 16384], P('tile'), may hold values from 0 to 1439
- obs_count: int32 [16], P('tile'), may hold values from 8192 to 16384, as said below
- innovation: float32 [16, 16384], P('tile'), may hold values from -12 to 12
- obs_weight: float32 [16, 16384], P('tile'), may hold values from 1 to 8
Outputs:
- gradient: bfloat16 [16, 16, 720, 1440], P('mem', None, 'tile')
The draws below stay inside these ranges and needn't reach their ends.
Inputs may be any that keep to these rules, and one draw needn't show every extreme that they name: Observations of band t fill slots 0 to obs_count[t] - 1; the other slots carry no observation. Some band is full in every draw.
All inputs are finite; a program needn't handle non-finite values.
Results may differ from the reference program's by a relative error of at most 0.0056.
Values may be sent and summed in bfloat16 or wider, within the bound.
No kernel may reach another device: no remote copies, remote signals or barrier semaphores. Data moves between devices by JAX's collectives and lax.ppermute only.
A program may use at most 128 MiB of HBM per device.

```python
import math
import jax
import jax.numpy as jnp
from jax import lax

NLON = 1440
NLAT = 720
LEV = 16
NOBS = 16384
MEMBERS = 16
TILES = 16
ROWS = 45


def draw_obs_count(key, part):
    first_key, second_key = jax.random.split(jax.random.fold_in(key, 7))
    counts = jax.random.randint(first_key, (TILES,), NOBS // 2, NOBS + 1)
    chosen = jax.random.randint(second_key, (), 0, TILES)
    return jnp.where(jnp.arange(TILES) == chosen, NOBS, counts).astype(jnp.int32)


def with_ends(result, key, smallest, top_value):
    shape = result.shape
    index_at = [jax.random.randint(jax.random.fold_in(key, axis), (), 0, shape[axis]) for axis in range(len(shape))]
    result = result.at[tuple(index_at)].set(smallest)
    longest = shape.index(max(shape))
    index_at[longest] = (index_at[longest] + 1) % shape[longest]
    return result.at[tuple(index_at)].set(top_value)


def steps_of(key, dims, cuts, least, top_value):
    gain = 1.0
    for position, blocks in cuts:
        heights = jax.random.uniform(jax.random.fold_in(jax.random.fold_in(key, 6), position), (blocks,), jnp.float32, least / len(cuts), top_value / len(cuts))
        gain = gain * jnp.repeat(jnp.exp(heights), dims[position] // blocks).reshape((-1,) + (1,) * (len(dims) - 1 - position))
    return gain


def bell_draw(own_key, dims, scale, limit, shards=(), kind=jnp.bfloat16):
    loudness = steps_of(own_key, dims, shards, -0.22, 0.18) if shards else 1.0
    drawn = jax.random.normal(own_key, dims, jnp.float32) * scale * loudness
    return jnp.minimum(jnp.maximum(drawn, -limit), limit).astype(kind)


def setup_inputs(seed: int = 0) -> dict:
    seeds = jax.random.split(jax.random.key(seed), 11)
    return {
        "alpha": bell_draw(seeds[0], (MEMBERS, LEV, NLAT, NLON), 1.0, 6.0, ((0, 16), (2, 16))),
        "perturbation": bell_draw(seeds[1], (MEMBERS, LEV, NLAT, NLON), 0.5, 3.0, ((0, 16), (2, 16))),
        "lon_scale": jnp.clip(jnp.exp(jax.random.uniform(seeds[2], (LEV,), jnp.float32, math.log(8.0), math.log(48.0))), 8.0, 48.0),
        "lat_scale": jnp.clip(jnp.exp(jax.random.uniform(seeds[3], (LEV,), jnp.float32, math.log(12.0), math.log(64.0))), 12.0, 64.0),
        "obs_level": with_ends(jax.random.randint(seeds[4], (TILES, NOBS), 0, LEV), jax.random.fold_in(seeds[4], 1), 0, LEV - 1).astype(jnp.int32),
        "obs_row": with_ends(jax.random.randint(seeds[5], (TILES, NOBS), 0, ROWS), jax.random.fold_in(seeds[5], 1), 0, ROWS - 1).astype(jnp.int32),
        "obs_col": with_ends(jax.random.randint(seeds[6], (TILES, NOBS), 0, NLON), jax.random.fold_in(seeds[6], 1), 0, NLON - 1).astype(jnp.int32),
        "obs_count": draw_obs_count(jax.random.fold_in(seeds[10], 71), 0),
        "innovation": bell_draw(seeds[8], (TILES, NOBS), 2.0, 12.0, ((0, 16),), jnp.float32),
        "obs_weight": jnp.clip(jnp.exp(math.log(8.0) - 2.0794415 * jax.random.uniform(seeds[9], (TILES, NOBS), jnp.float32) ** steps_of(seeds[9], (TILES, NOBS), ((0, 16),), -0.2, 0.2)), 1.0, 8.0),
    }


def square_root(lengths, extent, periodic):
    positions = jnp.arange(extent).astype(jnp.float32)
    distance = jnp.abs(positions[:, None] - positions[None, :])
    if periodic:
        distance = jnp.minimum(distance, extent - distance)
    scales = lengths[:, None, None]
    factor = (2.0 / jnp.pi) ** 0.25
    values = factor * jnp.exp(-(distance[None] / scales) ** 2) / jnp.sqrt(scales)
    return values.astype(jnp.bfloat16)

def reference(alpha, perturbation, lon_scale, lat_scale, obs_level, obs_row, obs_col, obs_count, innovation, obs_weight):
    lon_root = square_root(lon_scale, NLON, True).astype(jnp.float32)
    lat_root = square_root(lat_scale, NLAT, False).astype(jnp.float32)

    def localize(values_in):
        zonal = jnp.einsum('lab,lbc->lac', values_in, lon_root)
        zonal = lax.optimization_barrier(zonal.astype(jnp.bfloat16)).astype(jnp.float32)
        return jnp.einsum('lab,lbc->lac', lat_root, zonal)

    def forward(total, pair):
        member_alpha, member_pert = pair
        spread = lax.optimization_barrier(localize(member_alpha.astype(jnp.float32)).astype(jnp.bfloat16))
        return (total + member_pert.astype(jnp.float32) * spread.astype(jnp.float32), jnp.float32(0.0))
    start_field = jnp.zeros((LEV, NLAT, NLON), jnp.float32)
    increment = lax.scan(forward, start_field, (alpha, perturbation))[0]
    band_rows = (jnp.arange(TILES) * ROWS).astype(jnp.int32)[:, None] + obs_row
    model_obs = increment[obs_level, band_rows, obs_col]
    valid = jnp.arange(NOBS).astype(jnp.int32)[None, :] < obs_count[:, None]
    weighted = jnp.where(valid, obs_weight * (model_obs - innovation), 0.0).astype(jnp.float32)
    flat_index = (obs_level * NLAT + band_rows) * NLON + obs_col
    obs_field = jnp.zeros((LEV * NLAT * NLON,), jnp.float32).at[flat_index.reshape(-1)].add(weighted.reshape(-1))
    obs_field = obs_field.reshape(LEV, NLAT, NLON)

    def backward(carry, pair):
        member_alpha, member_pert = pair
        sensitive = lax.optimization_barrier((member_pert.astype(jnp.float32) * obs_field).astype(jnp.bfloat16))
        back_field = localize(sensitive.astype(jnp.float32))
        return (carry, (member_alpha.astype(jnp.float32) + back_field).astype(jnp.bfloat16))
    gradient = lax.scan(backward, jnp.float32(0.0), (alpha, perturbation))[1]
    return gradient
```

```python
import functools

import jax
import jax.numpy as jnp
from jax import lax
from jax.experimental import pallas as pl
from jax.experimental.pallas import tpu as pltpu
from jax.sharding import PartitionSpec as P

LANES = 128
BLOCK = 256
RUN_BLOCKS = 5
RUN = RUN_BLOCKS * BLOCK
PLANES = 8
SEND_ROWS = 24
F32 = jnp.float32
BF16 = jnp.bfloat16
VMEM = pltpu.VMEM
SMEM = pltpu.SMEM


def round_up(value, step):
    return (value + step - 1) // step * step


def square_root(lengths, place, valid, extent, periodic):
    position = place.astype(F32)
    distance = jnp.abs(position[:, None] - position[None, :])
    if periodic:
        distance = jnp.minimum(distance, extent - distance)
    factor = (2.0 / jnp.pi) ** 0.25
    values = factor * jnp.exp(-((distance / lengths) ** 2)) / jnp.sqrt(lengths)
    values = jnp.where(valid[:, None] & valid[None, :], values, 0.0)
    return values.astype(BF16)


def split_three(value):
    first = value.astype(BF16).astype(F32)
    rest = value - first
    second = rest.astype(BF16).astype(F32)
    return first, second, rest - second


def look_up(table_ref, group, cells, lane_iota, line_iota):
    width = table_ref.shape[2]
    lines = jnp.concatenate(
        [table_ref[group, :, BLOCK * part : BLOCK * (part + 1)] for part in range(width // BLOCK)],
        axis=0,
    )
    results = []
    for cell in cells:
        chosen = jnp.where(lane_iota == (cell & (BLOCK - 1)), 1.0, 0.0).astype(BF16)
        found = jnp.dot(lines, chosen, preferred_element_type=F32)
        results.append(
            jnp.sum(jnp.where(line_iota == (cell >> 8), found, 0.0), axis=0, keepdims=True)
        )
    return results


def run_cells(run_ref, group):
    return [run_ref[group, part : part + 1, :].astype(jnp.int32) for part in range(RUN_BLOCKS)]


def pack_kernel(
    scalar_ref, level_ref, cell_ref, weight_ref, innov_ref, table_ref, send_out, target_ref, plane_ref, total_ref
):
    levels, rows, width = table_ref.shape
    lines = level_ref.shape[0]
    places = levels * RUN_BLOCKS
    count = scalar_ref[0]
    first_rank = scalar_ref[1] * RUN
    slot = lax.broadcasted_iota(jnp.int32, (lines, LANES), 0) * LANES + lax.broadcasted_iota(
        jnp.int32, (lines, LANES), 1
    )
    level = jnp.where(slot < count, level_ref[...], levels)
    row_at = lax.broadcasted_iota(jnp.int32, (LANES, LANES), 0)
    lane_at = lax.broadcasted_iota(jnp.int32, (LANES, LANES), 1)
    upper = jnp.where(row_at <= lane_at, 1.0, 0.0).astype(BF16)
    ones = jnp.ones((LANES, LANES), BF16)
    before = jnp.where(
        lax.broadcasted_iota(jnp.int32, (lines, lines), 1)
        < lax.broadcasted_iota(jnp.int32, (lines, lines), 0),
        1.0,
        0.0,
    ).astype(BF16)
    rank = jnp.zeros((lines, LANES), F32)
    longest = jnp.zeros((1, LANES), F32)
    for index in range(levels):
        mask = level == index
        flags = jnp.where(mask, 1.0, 0.0).astype(BF16)
        inside = jnp.dot(flags, upper, preferred_element_type=F32)
        line_total = jnp.dot(flags, ones, preferred_element_type=F32)
        ahead = jnp.dot(before, line_total.astype(BF16), preferred_element_type=F32)
        rank = jnp.where(mask, ahead + inside - 1.0, rank)
        longest = jnp.maximum(longest, ahead[lines - 1 :, :] + line_total[lines - 1 :, :])
    place = rank.astype(jnp.int32) - first_rank
    kept = (level < levels) & (place >= 0) & (place < RUN)
    target_ref[...] = jnp.where(kept, level * RUN + place, -1)
    cell = cell_ref[...]
    plane_ref[0] = (cell & (BLOCK - 1)).astype(F32)
    plane_ref[1] = ((cell >> 8) - BLOCK // 2).astype(F32)
    for index, part in enumerate(split_three(weight_ref[...])):
        plane_ref[2 + index] = part
    for index, part in enumerate(split_three(innov_ref[...])):
        plane_ref[5 + index] = part
    total_ref[...] = jnp.zeros_like(total_ref)
    block_at = lax.broadcasted_iota(jnp.int32, (places, BLOCK), 0)
    lane_iota = lax.broadcasted_iota(jnp.int32, (BLOCK, BLOCK), 0)

    def pair_of(ref, index):
        return jnp.concatenate([ref[pl.ds(2 * index, 1), :], ref[pl.ds(2 * index + 1, 1), :]], axis=1)

    def place_block(index, carry):
        target = pair_of(target_ref, index)
        target_block = block_at == (target >> 8)
        target_lane = jnp.where(lane_iota == (target & (BLOCK - 1)), 1.0, 0.0).astype(BF16)
        parts = [
            jnp.where(target_block, pair_of(plane_ref.at[plane], index), 0.0).astype(BF16)
            for plane in range(PLANES)
        ]
        total_ref[...] += lax.dot_general(
            jnp.concatenate(parts, axis=0),
            target_lane,
            (((1,), (1,)), ((), ())),
            preferred_element_type=F32,
        )
        return carry

    lax.fori_loop(0, lines // 2, place_block, 0)
    planes = [total_ref[places * plane : places * (plane + 1), :] for plane in range(PLANES)]
    cell_sorted = (planes[1] + float(BLOCK // 2)) * float(BLOCK) + planes[0]
    weight_sorted = planes[2] + planes[3] + planes[4]
    innov_sorted = planes[5] + planes[6] + planes[7]
    tail = jnp.concatenate([longest] * (BLOCK // LANES), axis=1)
    for index in range(levels):
        run = slice(RUN_BLOCKS * index, RUN_BLOCKS * (index + 1))
        send_out[index, 0:RUN_BLOCKS, :] = cell_sorted[run]
        send_out[index, RUN_BLOCKS : 2 * RUN_BLOCKS, :] = weight_sorted[run]
        send_out[index, 2 * RUN_BLOCKS : 3 * RUN_BLOCKS, :] = innov_sorted[run]
        send_out[index, 4 * RUN_BLOCKS : SEND_ROWS, :] = jnp.broadcast_to(
            tail, (SEND_ROWS - 4 * RUN_BLOCKS, BLOCK)
        )
    line_iota = lax.broadcasted_iota(jnp.int32, (rows * width // BLOCK, BLOCK), 0)

    def one_level(index, carry):
        found = look_up(table_ref, index, run_cells(send_out, index), lane_iota, line_iota)
        for part in range(RUN_BLOCKS):
            send_out[index, 3 * RUN_BLOCKS + part : 3 * RUN_BLOCKS + part + 1, :] = found[part]
        return carry

    lax.fori_loop(0, levels, one_level, 0)


def pack_slots(scalars, level, cell, weight, innov, table):
    lines = level.shape[0]
    levels = table.shape[0]
    places = levels * RUN_BLOCKS
    whole = pl.BlockSpec(memory_space=VMEM)
    return pl.pallas_call(
        pack_kernel,
        out_shape=jax.ShapeDtypeStruct((levels, SEND_ROWS, BLOCK), F32),
        in_specs=[pl.BlockSpec(memory_space=SMEM)] + [whole] * 5,
        out_specs=whole,
        scratch_shapes=[
            VMEM((lines, LANES), jnp.int32),
            VMEM((PLANES, lines, LANES), F32),
            VMEM((PLANES * places, BLOCK), F32),
        ],
        compiler_params=pltpu.CompilerParams(vmem_limit_bytes=24 << 20),
        cost_estimate=pl.CostEstimate(flops=25 * 10**9, bytes_accessed=4 << 20, transcendentals=0),
        name="pack_slots",
    )(scalars, level, cell, weight, innov, table)


def term_kernel(table_ref, run_ref, term_out):
    groups, rows, width = table_ref.shape
    lane_iota = lax.broadcasted_iota(jnp.int32, (BLOCK, BLOCK), 0)
    line_iota = lax.broadcasted_iota(jnp.int32, (rows * width // BLOCK, BLOCK), 0)

    def one_group(group, carry):
        found = look_up(table_ref, group, run_cells(run_ref, group), lane_iota, line_iota)
        for part in range(RUN_BLOCKS):
            row = 3 * RUN_BLOCKS + part
            term_out[pl.ds(group * RUN_BLOCKS + part, 1), :] = (
                found[part] * run_ref[group, row : row + 1, :]
            )
        return carry

    lax.fori_loop(0, groups, one_group, 0)


def slot_terms(table, runs):
    groups = table.shape[0]
    whole = pl.BlockSpec(memory_space=VMEM)
    return pl.pallas_call(
        term_kernel,
        out_shape=jax.ShapeDtypeStruct((groups * RUN_BLOCKS, BLOCK), F32),
        in_specs=[whole, whole],
        out_specs=whole,
        compiler_params=pltpu.CompilerParams(vmem_limit_bytes=24 << 20),
        cost_estimate=pl.CostEstimate(flops=4 * 10**9, bytes_accessed=3 << 20, transcendentals=0),
        name="slot_terms",
    )(table, runs)


def add_kernel(run_ref, model_ref, field_out):
    groups, rows, width = field_out.shape
    parts = width // BLOCK
    lane_iota = lax.broadcasted_iota(jnp.int32, (BLOCK, RUN), 0)
    line_iota = lax.broadcasted_iota(jnp.int32, (rows * parts, RUN), 0)

    def one_group(group, carry):
        def row_of(first):
            return jnp.concatenate(
                [run_ref[group, first + part : first + part + 1, :] for part in range(RUN_BLOCKS)],
                axis=1,
            )

        cell = row_of(0).astype(jnp.int32)
        model = jnp.concatenate(
            [model_ref[pl.ds(group * RUN_BLOCKS + part, 1), :] for part in range(RUN_BLOCKS)], axis=1
        )
        weighted = row_of(RUN_BLOCKS) * (model - row_of(2 * RUN_BLOCKS))
        value = row_of(3 * RUN_BLOCKS) * weighted
        lines = jnp.where(line_iota == (cell >> 8), value, 0.0).astype(BF16)
        chosen = jnp.where(lane_iota == (cell & (BLOCK - 1)), 1.0, 0.0).astype(BF16)
        total = lax.dot_general(
            lines, chosen, (((1,), (1,)), ((), ())), preferred_element_type=F32
        )
        for part in range(parts):
            field_out[group, :, BLOCK * part : BLOCK * (part + 1)] = total[
                rows * part : rows * (part + 1), :
            ].astype(field_out.dtype)
        return carry

    lax.fori_loop(0, groups, one_group, 0)


def add_slots(runs, model, rows, width, dtype):
    groups = runs.shape[0]
    whole = pl.BlockSpec(memory_space=VMEM)
    return pl.pallas_call(
        add_kernel,
        out_shape=jax.ShapeDtypeStruct((groups, rows, width), dtype),
        in_specs=[whole, whole],
        out_specs=whole,
        compiler_params=pltpu.CompilerParams(vmem_limit_bytes=24 << 20),
        cost_estimate=pl.CostEstimate(flops=4 * 10**9, bytes_accessed=3 << 20, transcendentals=0),
        name="add_slots",
    )(runs, model)


def localize(values, lat_root, lon_root):
    zonal = jnp.dot(values, lon_root, preferred_element_type=F32).astype(BF16)
    return jnp.dot(lat_root, zonal, preferred_element_type=F32)


def sum_members(value):
    members = lax.axis_size("mem")
    step = 1
    while step < members:
        value = value + lax.ppermute(value, "mem", [(i, i ^ step) for i in range(members)])
        step *= 2
    return value


def exchange(value):
    return lax.all_to_all(value, "tile", split_axis=0, concat_axis=0, tiled=True)


def shards(
    alpha,
    perturbation,
    lon_scale,
    lat_scale,
    obs_level,
    obs_row,
    obs_col,
    obs_count,
    innovation,
    obs_weight,
):
    levels, rows, columns = alpha.shape[1:]
    tiles = lax.axis_size("tile")
    level = lax.axis_index("tile")
    slots = obs_level.shape[1]
    pad_rows = round_up(rows, 16)
    width = round_up(columns, BLOCK)
    padding = ((0, 0), (0, pad_rows - rows), (0, width - columns))

    alpha_slab = exchange(alpha[0])

    as_lines = lambda value: value.reshape(slots // LANES, LANES)
    column = as_lines(obs_col)
    cell = ((column >> 8) * pad_rows + as_lines(obs_row)) * BLOCK + (column & (BLOCK - 1))
    pert_table = jnp.pad(perturbation[0], padding)

    def packed_chunk(chunk):
        scalars = jnp.stack([obs_count[0], chunk])
        return pack_slots(
            scalars,
            as_lines(obs_level),
            cell,
            as_lines(obs_weight),
            as_lines(innovation),
            pert_table,
        )

    alpha_slab, packed = lax.optimization_barrier((alpha_slab, packed_chunk(jnp.int32(0))))
    runs = exchange(packed)
    longest = jnp.max(runs[:, SEND_ROWS - 1, 0]).astype(jnp.int32)

    column_at = jnp.arange(width)
    lon_root = square_root(
        lax.dynamic_index_in_dim(lon_scale, level, keepdims=False),
        column_at,
        column_at < columns,
        columns,
        True,
    )
    line = jnp.arange(tiles * pad_rows)
    row_in_band = line % pad_rows
    lat_root = square_root(
        lax.dynamic_index_in_dim(lat_scale, level, keepdims=False),
        (line // pad_rows) * rows + row_in_band,
        row_in_band < rows,
        rows * tiles,
        False,
    )
    lon_root, lat_root = lax.optimization_barrier((lon_root, lat_root))

    padded = jnp.pad(alpha_slab, padding).reshape(tiles * pad_rows, width)
    spread = localize(padded, lat_root, lon_root).astype(BF16).reshape(tiles, pad_rows, width)

    def chunk_field(chunk_run, dtype):
        model = sum_members(slot_terms(spread, chunk_run))
        return add_slots(chunk_run, model, pad_rows, width, dtype)

    def one_run():
        return chunk_field(runs, BF16)

    def many_runs():
        def one_chunk(chunk, field):
            return field + chunk_field(exchange(packed_chunk(chunk)), F32)

        start = jnp.zeros((tiles, pad_rows, width), F32)
        return lax.fori_loop(0, (longest + RUN - 1) // RUN, one_chunk, start).astype(BF16)

    sensitive = lax.cond(longest > RUN, many_runs, one_run)
    back = localize(sensitive.reshape(tiles * pad_rows, width), lat_root, lon_root)
    back = back.reshape(tiles, pad_rows, width)[:, :rows, :columns]
    gradient = (alpha_slab.astype(F32) + back).astype(BF16)
    return exchange(gradient)[None]


def solution(mesh):
    in_specs = (
        P("mem", None, "tile", None),
        P("mem", None, "tile", None),
        P(),
        P(),
        P("tile", None),
        P("tile", None),
        P("tile", None),
        P("tile"),
        P("tile", None),
        P("tile", None),
    )
    out_specs = P("mem", None, "tile", None)
    return jax.shard_map(shards, mesh=mesh, in_specs=in_specs, out_specs=out_specs, check_vma=False)
```

```python
import functools

import jax
import jax.numpy as jnp
from jax import lax
from jax.experimental import pallas as pl
from jax.experimental.pallas import tpu as pltpu
from jax.sharding import PartitionSpec as P

LANES = 128
BLOCK = 256
RUN_ROWS = 9
RUN = RUN_ROWS * LANES
PLANES = 8
SEND_ROWS = 40
ROW_STRIDE = 64
UNROLL = 4
F32 = jnp.float32
BF16 = jnp.bfloat16
VMEM = pltpu.VMEM
SMEM = pltpu.SMEM


def round_up(value, step):
    return (value + step - 1) // step * step


def square_root(lengths, place, valid, extent, periodic):
    position = place.astype(F32)
    distance = jnp.abs(position[:, None] - position[None, :])
    if periodic:
        distance = jnp.minimum(distance, extent - distance)
    factor = (2.0 / jnp.pi) ** 0.25
    values = factor * jnp.exp(-((distance / lengths) ** 2)) / jnp.sqrt(lengths)
    values = jnp.where(valid[:, None] & valid[None, :], values, 0.0)
    return values.astype(BF16)


def split_three(value):
    first = value.astype(BF16).astype(F32)
    rest = value - first
    second = rest.astype(BF16).astype(F32)
    return first, second, rest - second


def small_float(value):
    return value.astype(F32).astype(BF16)


def run_pieces(run_ref, group, first):
    rows = [run_ref[group, first + row : first + row + 1, :] for row in range(RUN_ROWS)]
    pieces = [
        jnp.concatenate(rows[row : row + 2], axis=1) for row in range(0, RUN_ROWS - 1, 2)
    ]
    return pieces + rows[RUN_ROWS - 1 :] if RUN_ROWS % 2 else pieces


def look_up(table_ref, group, cells, lane_index, row_index):
    rows, width = table_ref.shape[1:]
    parts = width // BLOCK
    lines = jnp.concatenate(
        [table_ref[group, :, BLOCK * part : BLOCK * (part + 1)] for part in range(parts)], axis=0
    )
    results = []
    for piece in cells:
        cell = piece.astype(jnp.int32)
        lanes = cell.shape[1]
        chosen = jnp.where(
            lane_index[:, :lanes] == small_float(cell & (BLOCK - 1)), jnp.ones((), BF16), jnp.zeros((), BF16)
        )
        found = jnp.dot(lines, chosen, preferred_element_type=F32)
        part_of = cell >> 14
        kept = found[0:rows]
        for part in range(1, parts):
            kept = jnp.where(part_of == part, found[rows * part : rows * (part + 1)], kept)
        row_of = (cell >> 8) & (ROW_STRIDE - 1)
        value = jnp.sum(
            jnp.where(row_index[:, :lanes] == row_of, kept, 0.0), axis=0, keepdims=True
        )
        for half in range(lanes // LANES):
            results.append(value[:, LANES * half : LANES * (half + 1)])
    return results


def look_up_indices(rows):
    lane_index = small_float(lax.broadcasted_iota(jnp.int32, (BLOCK, BLOCK), 0))
    row_index = lax.broadcasted_iota(jnp.int32, (rows, BLOCK), 0)
    return lane_index, row_index


def pack_kernel(
    scalar_ref, level_ref, cell_ref, weight_ref, innov_ref, table_ref, send_out, target_ref, plane_ref, total_ref
):
    levels, rows, width = table_ref.shape
    lines = level_ref.shape[0]
    places = levels * RUN // BLOCK
    count = scalar_ref[0]
    first_rank = scalar_ref[1] * RUN
    slot = lax.broadcasted_iota(jnp.int32, (lines, LANES), 0) * LANES + lax.broadcasted_iota(
        jnp.int32, (lines, LANES), 1
    )
    level = jnp.where(slot < count, level_ref[...], levels)
    row_at = lax.broadcasted_iota(jnp.int32, (LANES, LANES), 0)
    lane_at = lax.broadcasted_iota(jnp.int32, (LANES, LANES), 1)
    upper = jnp.where(row_at <= lane_at, 1.0, 0.0).astype(BF16)
    ones = jnp.ones((LANES, LANES), BF16)
    before = jnp.where(
        lax.broadcasted_iota(jnp.int32, (lines, lines), 1)
        < lax.broadcasted_iota(jnp.int32, (lines, lines), 0),
        1.0,
        0.0,
    ).astype(BF16)
    rank = jnp.zeros((lines, LANES), F32)
    longest = jnp.zeros((1, LANES), F32)
    for index in range(levels):
        mask = level == index
        flags = jnp.where(mask, 1.0, 0.0).astype(BF16)
        inside = jnp.dot(flags, upper, preferred_element_type=F32)
        line_total = jnp.dot(flags, ones, preferred_element_type=F32)
        ahead = jnp.dot(before, line_total.astype(BF16), preferred_element_type=F32)
        rank = jnp.where(mask, ahead + inside - 1.0, rank)
        longest = jnp.maximum(longest, ahead[lines - 1 :, :] + line_total[lines - 1 :, :])
    place = rank.astype(jnp.int32) - first_rank
    kept = (level < levels) & (place >= 0) & (place < RUN)
    target_ref[...] = jnp.where(kept, level * RUN + place, -1)
    cell = cell_ref[...]
    plane_ref[0] = (cell & (BLOCK - 1)).astype(F32)
    plane_ref[1] = ((cell >> 8) - BLOCK // 2).astype(F32)
    for index, part in enumerate(split_three(weight_ref[...])):
        plane_ref[2 + index] = part
    for index, part in enumerate(split_three(innov_ref[...])):
        plane_ref[5 + index] = part
    total_ref[...] = jnp.zeros_like(total_ref)
    block_at = lax.broadcasted_iota(jnp.int32, (places, BLOCK), 0)
    lane_iota = lax.broadcasted_iota(jnp.int32, (BLOCK, BLOCK), 0)

    def pair_of(ref, index):
        return jnp.concatenate([ref[pl.ds(2 * index, 1), :], ref[pl.ds(2 * index + 1, 1), :]], axis=1)

    def place_block(index, carry):
        target = pair_of(target_ref, index)
        target_block = block_at == (target >> 8)
        target_lane = jnp.where(lane_iota == (target & (BLOCK - 1)), 1.0, 0.0).astype(BF16)
        parts = [
            jnp.where(target_block, pair_of(plane_ref.at[plane], index), 0.0).astype(BF16)
            for plane in range(PLANES)
        ]
        total_ref[...] += lax.dot_general(
            jnp.concatenate(parts, axis=0),
            target_lane,
            (((1,), (1,)), ((), ())),
            preferred_element_type=F32,
        )
        return carry

    lax.fori_loop(0, lines // 2, place_block, 0)
    planes = [total_ref[places * plane : places * (plane + 1), :] for plane in range(PLANES)]
    cell_sorted = (planes[1] + float(BLOCK // 2)) * float(BLOCK) + planes[0]
    weight_sorted = planes[2] + planes[3] + planes[4]
    innov_sorted = planes[5] + planes[6] + planes[7]
    for index in range(levels):
        for row in range(RUN_ROWS):
            line, half = divmod(index * RUN_ROWS + row, BLOCK // LANES)
            for plane, piece in enumerate((cell_sorted, weight_sorted, innov_sorted)):
                at = plane * RUN_ROWS + row
                send_out[index, at : at + 1, :] = piece[
                    line : line + 1, LANES * half : LANES * (half + 1)
                ]
        send_out[index, 4 * RUN_ROWS : SEND_ROWS, :] = jnp.broadcast_to(
            longest, (SEND_ROWS - 4 * RUN_ROWS, LANES)
        )
    lane_index, row_index = look_up_indices(rows)

    def one_level(index, carry):
        found = look_up(table_ref, index, run_pieces(send_out, index, 0), lane_index, row_index)
        for row in range(RUN_ROWS):
            at = 3 * RUN_ROWS + row
            send_out[index, at : at + 1, :] = found[row]
        return carry

    lax.fori_loop(0, levels, one_level, 0, unroll=UNROLL)


def pack_slots(scalars, level, cell, weight, innov, table):
    lines = level.shape[0]
    levels = table.shape[0]
    places = levels * RUN // BLOCK
    whole = pl.BlockSpec(memory_space=VMEM)
    return pl.pallas_call(
        pack_kernel,
        out_shape=jax.ShapeDtypeStruct((levels, SEND_ROWS, LANES), F32),
        in_specs=[pl.BlockSpec(memory_space=SMEM)] + [whole] * 5,
        out_specs=whole,
        scratch_shapes=[
            VMEM((lines, LANES), jnp.int32),
            VMEM((PLANES, lines, LANES), F32),
            VMEM((PLANES * places, BLOCK), F32),
        ],
        compiler_params=pltpu.CompilerParams(vmem_limit_bytes=16 << 20),
        cost_estimate=pl.CostEstimate(flops=25 * 10**9, bytes_accessed=4 << 20, transcendentals=0),
        name="pack_slots",
    )(scalars, level, cell, weight, innov, table)


def term_kernel(table_ref, run_ref, term_out):
    groups, rows, width = table_ref.shape
    lane_index, row_index = look_up_indices(rows)

    def one_group(group, carry):
        found = look_up(table_ref, group, run_pieces(run_ref, group, 0), lane_index, row_index)
        for row in range(RUN_ROWS):
            at = 3 * RUN_ROWS + row
            term_out[pl.ds(group * RUN_ROWS + row, 1), :] = (
                found[row] * run_ref[group, at : at + 1, :]
            )
        return carry

    lax.fori_loop(0, groups, one_group, 0, unroll=UNROLL)


def slot_terms(table, runs):
    groups = table.shape[0]
    whole = pl.BlockSpec(memory_space=VMEM)
    return pl.pallas_call(
        term_kernel,
        out_shape=jax.ShapeDtypeStruct((groups * RUN_ROWS, LANES), F32),
        in_specs=[whole, whole],
        out_specs=whole,
        compiler_params=pltpu.CompilerParams(vmem_limit_bytes=12 << 20),
        cost_estimate=pl.CostEstimate(flops=4 * 10**9, bytes_accessed=3 << 20, transcendentals=0),
        name="slot_terms",
    )(table, runs)


def add_kernel(run_ref, model_ref, field_out):
    groups, rows, width = field_out.shape
    parts = width // BLOCK
    middle = ROW_STRIDE * parts // 2
    lane_index = small_float(lax.broadcasted_iota(jnp.int32, (BLOCK, RUN), 0))
    row_index = lax.broadcasted_iota(jnp.int32, (rows, RUN), 0)
    line_index = jnp.concatenate(
        [small_float(row_index + (ROW_STRIDE * part - middle)) for part in range(parts)], axis=0
    )

    def one_group(group, carry):
        def values_of(first):
            return jnp.concatenate(
                [run_ref[group, first + row : first + row + 1, :] for row in range(RUN_ROWS)], axis=1
            )

        cell = values_of(0).astype(jnp.int32)
        model = jnp.concatenate(
            [model_ref[pl.ds(group * RUN_ROWS + row, 1), :] for row in range(RUN_ROWS)], axis=1
        )
        weighted = values_of(RUN_ROWS) * (model - values_of(2 * RUN_ROWS))
        value = (values_of(3 * RUN_ROWS) * weighted).astype(BF16)
        lines = jnp.where(line_index == small_float((cell >> 8) - middle), value, jnp.zeros((), BF16))
        chosen = jnp.where(lane_index == small_float(cell & (BLOCK - 1)), jnp.ones((), BF16), jnp.zeros((), BF16))
        total = lax.dot_general(
            lines, chosen, (((1,), (1,)), ((), ())), preferred_element_type=F32
        )
        for part in range(parts):
            field_out[group, :, BLOCK * part : BLOCK * (part + 1)] = total[
                rows * part : rows * (part + 1), :
            ].astype(field_out.dtype)
        return carry

    lax.fori_loop(0, groups, one_group, 0, unroll=UNROLL)


def add_slots(runs, model, rows, width, dtype):
    groups = runs.shape[0]
    whole = pl.BlockSpec(memory_space=VMEM)
    return pl.pallas_call(
        add_kernel,
        out_shape=jax.ShapeDtypeStruct((groups, rows, width), dtype),
        in_specs=[whole, whole],
        out_specs=whole,
        compiler_params=pltpu.CompilerParams(vmem_limit_bytes=16 << 20),
        cost_estimate=pl.CostEstimate(flops=4 * 10**9, bytes_accessed=3 << 20, transcendentals=0),
        name="add_slots",
    )(runs, model)


def localize(values, lat_root, lon_root):
    zonal = jnp.dot(values, lon_root, preferred_element_type=F32).astype(BF16)
    return jnp.dot(lat_root, zonal, preferred_element_type=F32)


def sum_members(value):
    members = lax.axis_size("mem")
    step = 1
    while step < members:
        value = value + lax.ppermute(value, "mem", [(i, i ^ step) for i in range(members)])
        step *= 2
    return value


def exchange(value):
    return lax.all_to_all(value, "tile", split_axis=0, concat_axis=0, tiled=True)


def shards(
    alpha,
    perturbation,
    lon_scale,
    lat_scale,
    obs_level,
    obs_row,
    obs_col,
    obs_count,
    innovation,
    obs_weight,
):
    levels, rows, columns = alpha.shape[1:]
    tiles = lax.axis_size("tile")
    level = lax.axis_index("tile")
    slots = obs_level.shape[1]
    pad_rows = round_up(rows, 16)
    width = round_up(columns, BLOCK)
    padding = ((0, 0), (0, pad_rows - rows), (0, width - columns))

    alpha_slab = exchange(jnp.pad(alpha[0], padding))

    as_lines = lambda value: value.reshape(slots // LANES, LANES)
    column = as_lines(obs_col)
    cell = ((column >> 8) * ROW_STRIDE + as_lines(obs_row)) * BLOCK + (column & (BLOCK - 1))
    pert_table = jnp.pad(perturbation[0], padding)

    def packed_chunk(chunk):
        scalars = jnp.stack([obs_count[0], chunk])
        return pack_slots(
            scalars,
            as_lines(obs_level),
            cell,
            as_lines(obs_weight),
            as_lines(innovation),
            pert_table,
        )

    alpha_slab, packed = lax.optimization_barrier((alpha_slab, packed_chunk(jnp.int32(0))))
    runs = exchange(packed)
    longest = jnp.max(runs[:, SEND_ROWS - 1, 0]).astype(jnp.int32)

    column_at = jnp.arange(width)
    lon_root = square_root(
        lax.dynamic_index_in_dim(lon_scale, level, keepdims=False),
        column_at,
        column_at < columns,
        columns,
        True,
    )
    line = jnp.arange(tiles * pad_rows)
    row_in_band = line % pad_rows
    lat_root = square_root(
        lax.dynamic_index_in_dim(lat_scale, level, keepdims=False),
        (line // pad_rows) * rows + row_in_band,
        row_in_band < rows,
        rows * tiles,
        False,
    )
    lon_root, lat_root = lax.optimization_barrier((lon_root, lat_root))

    padded = alpha_slab.reshape(tiles * pad_rows, width)
    spread = localize(padded, lat_root, lon_root).astype(BF16).reshape(tiles, pad_rows, width)

    def chunk_field(chunk_run, dtype):
        model = sum_members(slot_terms(spread, chunk_run))
        return add_slots(chunk_run, model, pad_rows, width, dtype)

    def many_runs(_):
        def one_chunk(chunk, field):
            return field + chunk_field(exchange(packed_chunk(chunk)), F32)

        start = jnp.zeros((tiles, pad_rows, width), F32)
        return lax.fori_loop(0, (longest + RUN - 1) // RUN, one_chunk, start).astype(BF16)

    sensitive = lax.cond(longest > RUN, many_runs, lambda field: field, chunk_field(runs, BF16))
    back = localize(sensitive.reshape(tiles * pad_rows, width), lat_root, lon_root)
    gradient = (padded.astype(F32) + back).astype(BF16)
    return exchange(gradient.reshape(tiles, pad_rows, width))[None, :, :rows, :columns]


def solution(mesh):
    in_specs = (
        P("mem", None, "tile", None),
        P("mem", None, "tile", None),
        P(),
        P(),
        P("tile", None),
        P("tile", None),
        P("tile", None),
        P("tile"),
        P("tile", None),
        P("tile", None),
    )
    out_specs = P("mem", None, "tile", None)
    return jax.shard_map(shards, mesh=mesh, in_specs=in_specs, out_specs=out_specs, check_vma=False)
```

```python
import functools

import jax
import jax.numpy as jnp
from jax import lax
from jax.experimental import pallas as pl
from jax.experimental.pallas import tpu as pltpu
from jax.sharding import PartitionSpec as P

LANES = 128
BLOCK = 256
RUN_ROWS = 9
RUN = RUN_ROWS * LANES
PLANES = 8
SEND_ROWS = 40
ROW_STRIDE = 64
UNROLL = 4
F32 = jnp.float32
BF16 = jnp.bfloat16
VMEM = pltpu.VMEM
SMEM = pltpu.SMEM


def round_up(value, step):
    return (value + step - 1) // step * step


def square_root(lengths, place, valid, extent, periodic):
    position = place.astype(F32)
    distance = jnp.abs(position[:, None] - position[None, :])
    if periodic:
        distance = jnp.minimum(distance, extent - distance)
    factor = (2.0 / jnp.pi) ** 0.25
    values = factor * jnp.exp(-((distance / lengths) ** 2)) / jnp.sqrt(lengths)
    values = jnp.where(valid[:, None] & valid[None, :], values, 0.0)
    return values.astype(BF16)


def split_three(value):
    first = value.astype(BF16).astype(F32)
    rest = value - first
    second = rest.astype(BF16).astype(F32)
    return first, second, rest - second


def small_float(value):
    return value.astype(F32).astype(BF16)


def run_pieces(run_ref, group, first):
    rows = [run_ref[group, first + row : first + row + 1, :] for row in range(RUN_ROWS)]
    pieces = [
        jnp.concatenate(rows[row : row + 2], axis=1) for row in range(0, RUN_ROWS - 1, 2)
    ]
    return pieces + rows[RUN_ROWS - 1 :] if RUN_ROWS % 2 else pieces


def look_up(table_ref, group, cells, lane_index, row_index):
    rows, width = table_ref.shape[1:]
    parts = width // BLOCK
    lines = jnp.concatenate(
        [table_ref[group, :, BLOCK * part : BLOCK * (part + 1)] for part in range(parts)], axis=0
    )
    results = []
    for piece in cells:
        cell = piece.astype(jnp.int32)
        lanes = cell.shape[1]
        chosen = jnp.where(
            lane_index[:, :lanes] == small_float(cell & (BLOCK - 1)), jnp.ones((), BF16), jnp.zeros((), BF16)
        )
        found = jnp.dot(lines, chosen, preferred_element_type=F32)
        part_of = cell >> 14
        kept = found[0:rows]
        for part in range(1, parts):
            kept = jnp.where(part_of == part, found[rows * part : rows * (part + 1)], kept)
        row_of = (cell >> 8) & (ROW_STRIDE - 1)
        value = jnp.sum(
            jnp.where(row_index[:, :lanes] == row_of, kept, 0.0), axis=0, keepdims=True
        )
        for half in range(lanes // LANES):
            results.append(value[:, LANES * half : LANES * (half + 1)])
    return results


def look_up_indices(rows):
    lane_index = small_float(lax.broadcasted_iota(jnp.int32, (BLOCK, BLOCK), 0))
    row_index = lax.broadcasted_iota(jnp.int32, (rows, BLOCK), 0)
    return lane_index, row_index


def pack_kernel(
    scalar_ref, level_ref, cell_ref, weight_ref, innov_ref, table_ref, send_out, target_ref, plane_ref, total_ref
):
    levels, rows, width = table_ref.shape
    lines = level_ref.shape[0]
    places = levels * RUN // BLOCK
    count = scalar_ref[0]
    first_rank = scalar_ref[1] * RUN
    slot = lax.broadcasted_iota(jnp.int32, (lines, LANES), 0) * LANES + lax.broadcasted_iota(
        jnp.int32, (lines, LANES), 1
    )
    level = jnp.where(slot < count, level_ref[...], levels)
    row_at = lax.broadcasted_iota(jnp.int32, (LANES, LANES), 0)
    lane_at = lax.broadcasted_iota(jnp.int32, (LANES, LANES), 1)
    upper = jnp.where(row_at <= lane_at, 1.0, 0.0).astype(BF16)
    ones = jnp.ones((LANES, LANES), BF16)
    before = jnp.where(
        lax.broadcasted_iota(jnp.int32, (lines, lines), 1)
        < lax.broadcasted_iota(jnp.int32, (lines, lines), 0),
        1.0,
        0.0,
    ).astype(BF16)
    rank = jnp.zeros((lines, LANES), F32)
    longest = jnp.zeros((1, LANES), F32)
    for index in range(levels):
        mask = level == index
        flags = jnp.where(mask, 1.0, 0.0).astype(BF16)
        inside = jnp.dot(flags, upper, preferred_element_type=F32)
        line_total = jnp.dot(flags, ones, preferred_element_type=F32)
        ahead = jnp.dot(before, line_total.astype(BF16), preferred_element_type=F32)
        rank = jnp.where(mask, ahead + inside - 1.0, rank)
        longest = jnp.maximum(longest, ahead[lines - 1 :, :] + line_total[lines - 1 :, :])
    place = rank.astype(jnp.int32) - first_rank
    kept = (level < levels) & (place >= 0) & (place < RUN)
    target_ref[...] = jnp.where(kept, level * RUN + place, -1)
    cell = cell_ref[...]
    plane_ref[0] = (cell & (BLOCK - 1)).astype(F32)
    plane_ref[1] = ((cell >> 8) - BLOCK // 2).astype(F32)
    for index, part in enumerate(split_three(weight_ref[...])):
        plane_ref[2 + index] = part
    for index, part in enumerate(split_three(innov_ref[...])):
        plane_ref[5 + index] = part
    total_ref[...] = jnp.zeros_like(total_ref)
    block_at = lax.broadcasted_iota(jnp.int32, (places, BLOCK), 0)
    lane_iota = lax.broadcasted_iota(jnp.int32, (BLOCK, BLOCK), 0)

    def pair_of(ref, index):
        return jnp.concatenate([ref[pl.ds(2 * index, 1), :], ref[pl.ds(2 * index + 1, 1), :]], axis=1)

    def place_block(index, carry):
        target = pair_of(target_ref, index)
        target_block = block_at == (target >> 8)
        target_lane = jnp.where(lane_iota == (target & (BLOCK - 1)), 1.0, 0.0).astype(BF16)
        parts = [
            jnp.where(target_block, pair_of(plane_ref.at[plane], index), 0.0).astype(BF16)
            for plane in range(PLANES)
        ]
        total_ref[...] += lax.dot_general(
            jnp.concatenate(parts, axis=0),
            target_lane,
            (((1,), (1,)), ((), ())),
            preferred_element_type=F32,
        )
        return carry

    lax.fori_loop(0, lines // 2, place_block, 0)
    planes = [total_ref[places * plane : places * (plane + 1), :] for plane in range(PLANES)]
    cell_sorted = (planes[1] + float(BLOCK // 2)) * float(BLOCK) + planes[0]
    weight_sorted = planes[2] + planes[3] + planes[4]
    innov_sorted = planes[5] + planes[6] + planes[7]
    for index in range(levels):
        for row in range(RUN_ROWS):
            line, half = divmod(index * RUN_ROWS + row, BLOCK // LANES)
            for plane, piece in enumerate((cell_sorted, weight_sorted, innov_sorted)):
                at = plane * RUN_ROWS + row
                send_out[index, at : at + 1, :] = piece[
                    line : line + 1, LANES * half : LANES * (half + 1)
                ]
        send_out[index, 4 * RUN_ROWS : SEND_ROWS, :] = jnp.broadcast_to(
            longest, (SEND_ROWS - 4 * RUN_ROWS, LANES)
        )
    lane_index, row_index = look_up_indices(rows)

    def one_level(index, carry):
        found = look_up(table_ref, index, run_pieces(send_out, index, 0), lane_index, row_index)
        for row in range(RUN_ROWS):
            at = 3 * RUN_ROWS + row
            send_out[index, at : at + 1, :] = found[row]
        return carry

    lax.fori_loop(0, levels, one_level, 0, unroll=UNROLL)


def pack_slots(scalars, level, cell, weight, innov, table):
    lines = level.shape[0]
    levels = table.shape[0]
    places = levels * RUN // BLOCK
    whole = pl.BlockSpec(memory_space=VMEM)
    return pl.pallas_call(
        pack_kernel,
        out_shape=jax.ShapeDtypeStruct((levels, SEND_ROWS, LANES), F32),
        in_specs=[pl.BlockSpec(memory_space=SMEM)] + [whole] * 5,
        out_specs=whole,
        scratch_shapes=[
            VMEM((lines, LANES), jnp.int32),
            VMEM((PLANES, lines, LANES), F32),
            VMEM((PLANES * places, BLOCK), F32),
        ],
        compiler_params=pltpu.CompilerParams(vmem_limit_bytes=16 << 20),
        cost_estimate=pl.CostEstimate(flops=25 * 10**9, bytes_accessed=4 << 20, transcendentals=0),
        name="pack_slots",
    )(scalars, level, cell, weight, innov, table)


def term_kernel(table_ref, run_ref, term_out):
    groups, rows, width = table_ref.shape
    lane_index, row_index = look_up_indices(rows)

    def one_group(group, carry):
        found = look_up(table_ref, group, run_pieces(run_ref, group, 0), lane_index, row_index)
        for row in range(RUN_ROWS):
            at = 3 * RUN_ROWS + row
            term_out[pl.ds(group * RUN_ROWS + row, 1), :] = (
                found[row] * run_ref[group, at : at + 1, :]
            )
        return carry

    lax.fori_loop(0, groups, one_group, 0, unroll=UNROLL)


def slot_terms(table, runs):
    groups = table.shape[0]
    whole = pl.BlockSpec(memory_space=VMEM)
    return pl.pallas_call(
        term_kernel,
        out_shape=jax.ShapeDtypeStruct((groups * RUN_ROWS, LANES), F32),
        in_specs=[whole, whole],
        out_specs=whole,
        compiler_params=pltpu.CompilerParams(vmem_limit_bytes=12 << 20),
        cost_estimate=pl.CostEstimate(flops=4 * 10**9, bytes_accessed=3 << 20, transcendentals=0),
        name="slot_terms",
    )(table, runs)


def add_kernel(run_ref, model_ref, field_out):
    groups, rows, width = field_out.shape
    parts = width // BLOCK
    middle = ROW_STRIDE * parts // 2
    lane_index = small_float(lax.broadcasted_iota(jnp.int32, (BLOCK, RUN), 0))
    row_index = lax.broadcasted_iota(jnp.int32, (rows, RUN), 0)
    line_index = jnp.concatenate(
        [small_float(row_index + (ROW_STRIDE * part - middle)) for part in range(parts)], axis=0
    )

    def one_group(group, carry):
        def values_of(first):
            return jnp.concatenate(
                [run_ref[group, first + row : first + row + 1, :] for row in range(RUN_ROWS)], axis=1
            )

        cell = values_of(0).astype(jnp.int32)
        model = jnp.concatenate(
            [model_ref[pl.ds(group * RUN_ROWS + row, 1), :] for row in range(RUN_ROWS)], axis=1
        )
        weighted = values_of(RUN_ROWS) * (model - values_of(2 * RUN_ROWS))
        value = (values_of(3 * RUN_ROWS) * weighted).astype(BF16)
        lines = jnp.where(line_index == small_float((cell >> 8) - middle), value, jnp.zeros((), BF16))
        chosen = jnp.where(lane_index == small_float(cell & (BLOCK - 1)), jnp.ones((), BF16), jnp.zeros((), BF16))
        total = lax.dot_general(
            lines, chosen, (((1,), (1,)), ((), ())), preferred_element_type=F32
        )
        for part in range(parts):
            field_out[group, :, BLOCK * part : BLOCK * (part + 1)] = total[
                rows * part : rows * (part + 1), :
            ].astype(field_out.dtype)
        return carry

    lax.fori_loop(0, groups, one_group, 0, unroll=UNROLL)


def add_slots(runs, model, rows, width, dtype):
    groups = runs.shape[0]
    whole = pl.BlockSpec(memory_space=VMEM)
    return pl.pallas_call(
        add_kernel,
        out_shape=jax.ShapeDtypeStruct((groups, rows, width), dtype),
        in_specs=[whole, whole],
        out_specs=whole,
        compiler_params=pltpu.CompilerParams(vmem_limit_bytes=16 << 20),
        cost_estimate=pl.CostEstimate(flops=4 * 10**9, bytes_accessed=3 << 20, transcendentals=0),
        name="add_slots",
    )(runs, model)


def localize(values, lat_root, lon_root):
    zonal = jnp.dot(values, lon_root, preferred_element_type=F32).astype(BF16)
    return jnp.dot(lat_root, zonal, preferred_element_type=F32)


def sum_members(value):
    members = lax.axis_size("mem")
    step = 1
    while step < members:
        value = value + lax.ppermute(value, "mem", [(i, i ^ step) for i in range(members)])
        step *= 2
    return value


def exchange(value):
    return lax.all_to_all(value, "tile", split_axis=0, concat_axis=0, tiled=True)


def shards(
    alpha,
    perturbation,
    lon_scale,
    lat_scale,
    obs_level,
    obs_row,
    obs_col,
    obs_count,
    innovation,
    obs_weight,
):
    levels, rows, columns = alpha.shape[1:]
    tiles = lax.axis_size("tile")
    level = lax.axis_index("tile")
    slots = obs_level.shape[1]
    pad_rows = round_up(rows, 16)
    width = round_up(columns, BLOCK)
    padding = ((0, 0), (0, pad_rows - rows), (0, width - columns))

    alpha_slab = exchange(jnp.pad(alpha[0], padding))

    as_lines = lambda value: value.reshape(slots // LANES, LANES)
    column = as_lines(obs_col)
    cell = ((column >> 8) * ROW_STRIDE + as_lines(obs_row)) * BLOCK + (column & (BLOCK - 1))
    pert_table = jnp.pad(perturbation[0], padding)

    def packed_chunk(chunk):
        scalars = jnp.stack([obs_count[0], chunk])
        return pack_slots(
            scalars,
            as_lines(obs_level),
            cell,
            as_lines(obs_weight),
            as_lines(innovation),
            pert_table,
        )

    alpha_slab, packed = lax.optimization_barrier((alpha_slab, packed_chunk(jnp.int32(0))))
    runs = exchange(packed)
    longest = jnp.max(runs[:, SEND_ROWS - 1, 0]).astype(jnp.int32)

    column_at = jnp.arange(width)
    lon_root = square_root(
        lax.dynamic_index_in_dim(lon_scale, level, keepdims=False),
        column_at,
        column_at < columns,
        columns,
        True,
    )
    line = jnp.arange(tiles * pad_rows)
    row_in_band = line % pad_rows
    lat_root = square_root(
        lax.dynamic_index_in_dim(lat_scale, level, keepdims=False),
        (line // pad_rows) * rows + row_in_band,
        row_in_band < rows,
        rows * tiles,
        False,
    )
    lon_root, lat_root = lax.optimization_barrier((lon_root, lat_root))

    padded = alpha_slab.reshape(tiles * pad_rows, width)
    spread = localize(padded, lat_root, lon_root).astype(BF16).reshape(tiles, pad_rows, width)

    def chunk_field(chunk_run, dtype):
        model = sum_members(slot_terms(spread, chunk_run))
        return add_slots(chunk_run, model, pad_rows, width, dtype)

    def gradient_of(field):
        back = localize(field.reshape(tiles * pad_rows, width), lat_root, lon_root)
        return (padded.astype(F32) + back).astype(BF16).reshape(tiles, pad_rows, width)

    def many_runs(_):
        def one_chunk(chunk, field):
            return field + chunk_field(exchange(packed_chunk(chunk)), F32)

        start = jnp.zeros((tiles, pad_rows, width), F32)
        chunks = (longest + RUN - 1) // RUN
        return gradient_of(lax.fori_loop(0, chunks, one_chunk, start).astype(BF16))

    first = lax.optimization_barrier(gradient_of(chunk_field(runs, BF16)))
    gradient = lax.cond(longest > RUN, many_runs, lambda done: done, first)
    return exchange(gradient)[None, :, :rows, :columns]


def solution(mesh):
    in_specs = (
        P("mem", None, "tile", None),
        P("mem", None, "tile", None),
        P(),
        P(),
        P("tile", None),
        P("tile", None),
        P("tile", None),
        P("tile"),
        P("tile", None),
        P("tile", None),
    )
    out_specs = P("mem", None, "tile", None)
    return jax.shard_map(shards, mesh=mesh, in_specs=in_specs, out_specs=out_specs, check_vma=False)
```

```python
import functools

import jax
import jax.numpy as jnp
from jax import lax
from jax.experimental import pallas as pl
from jax.experimental.pallas import tpu as pltpu
from jax.sharding import PartitionSpec as P

LANES = 128
BLOCK = 256
RUN_ROWS = 9
RUN = RUN_ROWS * LANES
PLANES = 8
SEND_ROWS = 40
ROW_STRIDE = 64
UNROLL = 4
SLAB_UNROLL = 8
F32 = jnp.float32
BF16 = jnp.bfloat16
VMEM = pltpu.VMEM
SMEM = pltpu.SMEM


def round_up(value, step):
    return (value + step - 1) // step * step


def square_root(lengths, place, valid, extent, periodic):
    position = place.astype(F32)
    distance = jnp.abs(position[:, None] - position[None, :])
    if periodic:
        distance = jnp.minimum(distance, extent - distance)
    factor = (2.0 / jnp.pi) ** 0.25
    values = factor * jnp.exp(-((distance / lengths) ** 2)) / jnp.sqrt(lengths)
    values = jnp.where(valid[:, None] & valid[None, :], values, 0.0)
    return values.astype(BF16)


def split_three(value):
    first = value.astype(BF16).astype(F32)
    rest = value - first
    second = rest.astype(BF16).astype(F32)
    return first, second, rest - second


def small_float(value):
    return value.astype(F32).astype(BF16)


def run_pieces(run_ref, group, first):
    rows = [run_ref[group, first + row : first + row + 1, :] for row in range(RUN_ROWS)]
    pieces = [
        jnp.concatenate(rows[row : row + 2], axis=1) for row in range(0, RUN_ROWS - 1, 2)
    ]
    return pieces + rows[RUN_ROWS - 1 :] if RUN_ROWS % 2 else pieces


def look_up(table_ref, group, cells, lane_index, row_index):
    rows, width = table_ref.shape[1:]
    parts = width // BLOCK
    lines = jnp.concatenate(
        [table_ref[group, :, BLOCK * part : BLOCK * (part + 1)] for part in range(parts)], axis=0
    )
    results = []
    for piece in cells:
        cell = piece.astype(jnp.int32)
        lanes = cell.shape[1]
        chosen = jnp.where(
            lane_index[:, :lanes] == small_float(cell & (BLOCK - 1)), jnp.ones((), BF16), jnp.zeros((), BF16)
        )
        found = jnp.dot(lines, chosen, preferred_element_type=F32)
        part_of = cell >> 14
        kept = found[0:rows]
        for part in range(1, parts):
            kept = jnp.where(part_of == part, found[rows * part : rows * (part + 1)], kept)
        row_of = (cell >> 8) & (ROW_STRIDE - 1)
        value = jnp.sum(
            jnp.where(row_index[:, :lanes] == row_of, kept, 0.0), axis=0, keepdims=True
        )
        for half in range(lanes // LANES):
            results.append(value[:, LANES * half : LANES * (half + 1)])
    return results


def look_up_indices(rows):
    lane_index = small_float(lax.broadcasted_iota(jnp.int32, (BLOCK, BLOCK), 0))
    row_index = lax.broadcasted_iota(jnp.int32, (rows, BLOCK), 0)
    return lane_index, row_index


def pack_kernel(
    scalar_ref, level_ref, cell_ref, weight_ref, innov_ref, table_ref, send_out, target_ref, plane_ref, total_ref
):
    levels, rows, width = table_ref.shape
    lines = level_ref.shape[0]
    places = levels * RUN // BLOCK
    count = scalar_ref[0]
    first_rank = scalar_ref[1] * RUN
    slot = lax.broadcasted_iota(jnp.int32, (lines, LANES), 0) * LANES + lax.broadcasted_iota(
        jnp.int32, (lines, LANES), 1
    )
    level = jnp.where(slot < count, level_ref[...], levels)
    row_at = lax.broadcasted_iota(jnp.int32, (LANES, LANES), 0)
    lane_at = lax.broadcasted_iota(jnp.int32, (LANES, LANES), 1)
    upper = jnp.where(row_at <= lane_at, 1.0, 0.0).astype(BF16)
    ones = jnp.ones((LANES, LANES), BF16)
    before = jnp.where(
        lax.broadcasted_iota(jnp.int32, (lines, lines), 1)
        < lax.broadcasted_iota(jnp.int32, (lines, lines), 0),
        1.0,
        0.0,
    ).astype(BF16)
    rank = jnp.zeros((lines, LANES), F32)
    longest = jnp.zeros((1, LANES), F32)
    for index in range(levels):
        mask = level == index
        flags = jnp.where(mask, 1.0, 0.0).astype(BF16)
        inside = jnp.dot(flags, upper, preferred_element_type=F32)
        line_total = jnp.dot(flags, ones, preferred_element_type=F32)
        ahead = jnp.dot(before, line_total.astype(BF16), preferred_element_type=F32)
        rank = jnp.where(mask, ahead + inside - 1.0, rank)
        longest = jnp.maximum(longest, ahead[lines - 1 :, :] + line_total[lines - 1 :, :])
    place = rank.astype(jnp.int32) - first_rank
    kept = (level < levels) & (place >= 0) & (place < RUN)
    target_ref[...] = jnp.where(kept, level * RUN + place, -1)
    cell = cell_ref[...]
    plane_ref[0] = (cell & (BLOCK - 1)).astype(F32)
    plane_ref[1] = ((cell >> 8) - BLOCK // 2).astype(F32)
    for index, part in enumerate(split_three(weight_ref[...])):
        plane_ref[2 + index] = part
    for index, part in enumerate(split_three(innov_ref[...])):
        plane_ref[5 + index] = part
    total_ref[...] = jnp.zeros_like(total_ref)
    block_at = lax.broadcasted_iota(jnp.int32, (places, BLOCK), 0)
    lane_iota = lax.broadcasted_iota(jnp.int32, (BLOCK, BLOCK), 0)

    def pair_of(ref, index):
        return jnp.concatenate([ref[pl.ds(2 * index, 1), :], ref[pl.ds(2 * index + 1, 1), :]], axis=1)

    def place_block(index, carry):
        target = pair_of(target_ref, index)
        target_block = block_at == (target >> 8)
        target_lane = jnp.where(lane_iota == (target & (BLOCK - 1)), 1.0, 0.0).astype(BF16)
        parts = [
            jnp.where(target_block, pair_of(plane_ref.at[plane], index), 0.0).astype(BF16)
            for plane in range(PLANES)
        ]
        total_ref[...] += lax.dot_general(
            jnp.concatenate(parts, axis=0),
            target_lane,
            (((1,), (1,)), ((), ())),
            preferred_element_type=F32,
        )
        return carry

    lax.fori_loop(0, lines // 2, place_block, 0)
    planes = [total_ref[places * plane : places * (plane + 1), :] for plane in range(PLANES)]
    cell_sorted = (planes[1] + float(BLOCK // 2)) * float(BLOCK) + planes[0]
    weight_sorted = planes[2] + planes[3] + planes[4]
    innov_sorted = planes[5] + planes[6] + planes[7]
    for index in range(levels):
        for row in range(RUN_ROWS):
            line, half = divmod(index * RUN_ROWS + row, BLOCK // LANES)
            for plane, piece in enumerate((cell_sorted, weight_sorted, innov_sorted)):
                at = plane * RUN_ROWS + row
                send_out[index, at : at + 1, :] = piece[
                    line : line + 1, LANES * half : LANES * (half + 1)
                ]
        send_out[index, 4 * RUN_ROWS : SEND_ROWS, :] = jnp.broadcast_to(
            longest, (SEND_ROWS - 4 * RUN_ROWS, LANES)
        )
    lane_index, row_index = look_up_indices(rows)

    def one_level(index, carry):
        found = look_up(table_ref, index, run_pieces(send_out, index, 0), lane_index, row_index)
        for row in range(RUN_ROWS):
            at = 3 * RUN_ROWS + row
            send_out[index, at : at + 1, :] = found[row]
        return carry

    lax.fori_loop(0, levels, one_level, 0, unroll=UNROLL)


def pack_slots(scalars, level, cell, weight, innov, table):
    lines = level.shape[0]
    levels = table.shape[0]
    places = levels * RUN // BLOCK
    whole = pl.BlockSpec(memory_space=VMEM)
    return pl.pallas_call(
        pack_kernel,
        out_shape=jax.ShapeDtypeStruct((levels, SEND_ROWS, LANES), F32),
        in_specs=[pl.BlockSpec(memory_space=SMEM)] + [whole] * 5,
        out_specs=whole,
        scratch_shapes=[
            VMEM((lines, LANES), jnp.int32),
            VMEM((PLANES, lines, LANES), F32),
            VMEM((PLANES * places, BLOCK), F32),
        ],
        compiler_params=pltpu.CompilerParams(vmem_limit_bytes=16 << 20),
        cost_estimate=pl.CostEstimate(flops=25 * 10**9, bytes_accessed=4 << 20, transcendentals=0),
        name="pack_slots",
    )(scalars, level, cell, weight, innov, table)


def term_kernel(table_ref, run_ref, term_out):
    groups, rows, width = table_ref.shape
    lane_index, row_index = look_up_indices(rows)

    def one_group(group, carry):
        found = look_up(table_ref, group, run_pieces(run_ref, group, 0), lane_index, row_index)
        for row in range(RUN_ROWS):
            at = 3 * RUN_ROWS + row
            term_out[pl.ds(group * RUN_ROWS + row, 1), :] = (
                found[row] * run_ref[group, at : at + 1, :]
            )
        return carry

    lax.fori_loop(0, groups, one_group, 0, unroll=SLAB_UNROLL)


def slot_terms(table, runs):
    groups = table.shape[0]
    whole = pl.BlockSpec(memory_space=VMEM)
    return pl.pallas_call(
        term_kernel,
        out_shape=jax.ShapeDtypeStruct((groups * RUN_ROWS, LANES), F32),
        in_specs=[whole, whole],
        out_specs=whole,
        compiler_params=pltpu.CompilerParams(vmem_limit_bytes=12 << 20),
        cost_estimate=pl.CostEstimate(flops=4 * 10**9, bytes_accessed=3 << 20, transcendentals=0),
        name="slot_terms",
    )(table, runs)


def add_kernel(run_ref, model_ref, field_out):
    groups, rows, width = field_out.shape
    parts = width // BLOCK
    middle = ROW_STRIDE * parts // 2
    lane_index = small_float(lax.broadcasted_iota(jnp.int32, (BLOCK, RUN), 0))
    row_index = lax.broadcasted_iota(jnp.int32, (rows, RUN), 0)
    line_index = jnp.concatenate(
        [small_float(row_index + (ROW_STRIDE * part - middle)) for part in range(parts)], axis=0
    )

    def one_group(group, carry):
        def values_of(first):
            return jnp.concatenate(
                [run_ref[group, first + row : first + row + 1, :] for row in range(RUN_ROWS)], axis=1
            )

        cell = values_of(0).astype(jnp.int32)
        model = jnp.concatenate(
            [model_ref[pl.ds(group * RUN_ROWS + row, 1), :] for row in range(RUN_ROWS)], axis=1
        )
        weighted = values_of(RUN_ROWS) * (model - values_of(2 * RUN_ROWS))
        value = (values_of(3 * RUN_ROWS) * weighted).astype(BF16)
        lines = jnp.where(line_index == small_float((cell >> 8) - middle), value, jnp.zeros((), BF16))
        chosen = jnp.where(lane_index == small_float(cell & (BLOCK - 1)), jnp.ones((), BF16), jnp.zeros((), BF16))
        total = lax.dot_general(
            lines, chosen, (((1,), (1,)), ((), ())), preferred_element_type=F32
        )
        for part in range(parts):
            field_out[group, :, BLOCK * part : BLOCK * (part + 1)] = total[
                rows * part : rows * (part + 1), :
            ].astype(field_out.dtype)
        return carry

    lax.fori_loop(0, groups, one_group, 0, unroll=SLAB_UNROLL)


def add_slots(runs, model, rows, width, dtype):
    groups = runs.shape[0]
    whole = pl.BlockSpec(memory_space=VMEM)
    return pl.pallas_call(
        add_kernel,
        out_shape=jax.ShapeDtypeStruct((groups, rows, width), dtype),
        in_specs=[whole, whole],
        out_specs=whole,
        compiler_params=pltpu.CompilerParams(vmem_limit_bytes=16 << 20),
        cost_estimate=pl.CostEstimate(flops=4 * 10**9, bytes_accessed=3 << 20, transcendentals=0),
        name="add_slots",
    )(runs, model)


def localize(values, lat_root, lon_root):
    zonal = jnp.dot(values, lon_root, preferred_element_type=F32).astype(BF16)
    return jnp.dot(lat_root, zonal, preferred_element_type=F32)


def sum_members(value):
    members = lax.axis_size("mem")
    step = 1
    while step < members:
        value = value + lax.ppermute(value, "mem", [(i, i ^ step) for i in range(members)])
        step *= 2
    return value


def exchange(value):
    return lax.all_to_all(value, "tile", split_axis=0, concat_axis=0, tiled=True)


def shards(
    alpha,
    perturbation,
    lon_scale,
    lat_scale,
    obs_level,
    obs_row,
    obs_col,
    obs_count,
    innovation,
    obs_weight,
):
    levels, rows, columns = alpha.shape[1:]
    tiles = lax.axis_size("tile")
    level = lax.axis_index("tile")
    slots = obs_level.shape[1]
    pad_rows = round_up(rows, 16)
    width = round_up(columns, BLOCK)
    padding = ((0, 0), (0, pad_rows - rows), (0, width - columns))

    alpha_slab = exchange(jnp.pad(alpha[0], padding))

    as_lines = lambda value: value.reshape(slots // LANES, LANES)
    column = as_lines(obs_col)
    cell = ((column >> 8) * ROW_STRIDE + as_lines(obs_row)) * BLOCK + (column & (BLOCK - 1))
    pert_table = jnp.pad(perturbation[0], padding)

    def packed_chunk(chunk):
        scalars = jnp.stack([obs_count[0], chunk])
        return pack_slots(
            scalars,
            as_lines(obs_level),
            cell,
            as_lines(obs_weight),
            as_lines(innovation),
            pert_table,
        )

    alpha_slab, packed = lax.optimization_barrier((alpha_slab, packed_chunk(jnp.int32(0))))
    runs = exchange(packed)
    longest = jnp.max(runs[:, SEND_ROWS - 1, 0]).astype(jnp.int32)

    column_at = jnp.arange(width)
    lon_root = square_root(
        lax.dynamic_index_in_dim(lon_scale, level, keepdims=False),
        column_at,
        column_at < columns,
        columns,
        True,
    )
    line = jnp.arange(tiles * pad_rows)
    row_in_band = line % pad_rows
    lat_root = square_root(
        lax.dynamic_index_in_dim(lat_scale, level, keepdims=False),
        (line // pad_rows) * rows + row_in_band,
        row_in_band < rows,
        rows * tiles,
        False,
    )
    lon_root, lat_root = lax.optimization_barrier((lon_root, lat_root))

    padded = alpha_slab.reshape(tiles * pad_rows, width)
    spread = localize(padded, lat_root, lon_root).astype(BF16).reshape(tiles, pad_rows, width)

    def chunk_field(chunk_run, dtype):
        model = sum_members(slot_terms(spread, chunk_run))
        return add_slots(chunk_run, model, pad_rows, width, dtype)

    def gradient_of(field):
        back = localize(field.reshape(tiles * pad_rows, width), lat_root, lon_root)
        return (padded.astype(F32) + back).astype(BF16).reshape(tiles, pad_rows, width)

    def many_runs(_):
        def one_chunk(chunk, field):
            return field + chunk_field(exchange(packed_chunk(chunk)), F32)

        start = jnp.zeros((tiles, pad_rows, width), F32)
        chunks = (longest + RUN - 1) // RUN
        return gradient_of(lax.fori_loop(0, chunks, one_chunk, start).astype(BF16))

    first = lax.optimization_barrier(gradient_of(chunk_field(runs, BF16)))
    gradient = lax.cond(longest > RUN, many_runs, lambda done: done, first)
    return exchange(gradient)[None, :, :rows, :columns]


def solution(mesh):
    in_specs = (
        P("mem", None, "tile", None),
        P("mem", None, "tile", None),
        P(),
        P(),
        P("tile", None),
        P("tile", None),
        P("tile", None),
        P("tile"),
        P("tile", None),
        P("tile", None),
    )
    out_specs = P("mem", None, "tile", None)
    return jax.shard_map(shards, mesh=mesh, in_specs=in_specs, out_specs=out_specs, check_vma=False)
```

```python
import functools

import jax
import jax.numpy as jnp
from jax import lax
from jax.experimental import pallas as pl
from jax.experimental.pallas import tpu as pltpu
from jax.sharding import PartitionSpec as P

LANES = 128
BLOCK = 256
RUN_ROWS = 9
RUN = RUN_ROWS * LANES
PLANES = 8
SEND_ROWS = 40
ROW_STRIDE = 64
UNROLL = 4
SLAB_UNROLL = 8
F32 = jnp.float32
BF16 = jnp.bfloat16
VMEM = pltpu.VMEM
SMEM = pltpu.SMEM


def round_up(value, step):
    return (value + step - 1) // step * step


def square_root(lengths, place, valid, extent, periodic):
    position = place.astype(F32)
    distance = jnp.abs(position[:, None] - position[None, :])
    if periodic:
        distance = jnp.minimum(distance, extent - distance)
    factor = (2.0 / jnp.pi) ** 0.25
    values = factor * jnp.exp(-((distance / lengths) ** 2)) / jnp.sqrt(lengths)
    values = jnp.where(valid[:, None] & valid[None, :], values, 0.0)
    return values.astype(BF16)


def split_three(value):
    first = value.astype(BF16).astype(F32)
    rest = value - first
    second = rest.astype(BF16).astype(F32)
    return first, second, rest - second


def small_float(value):
    return value.astype(F32).astype(BF16)


def run_pieces(run_ref, group, first):
    rows = [run_ref[group, first + row : first + row + 1, :] for row in range(RUN_ROWS)]
    pieces = [
        jnp.concatenate(rows[row : row + 2], axis=1) for row in range(0, RUN_ROWS - 1, 2)
    ]
    return pieces + rows[RUN_ROWS - 1 :] if RUN_ROWS % 2 else pieces


def look_up(table_ref, group, cells, lane_index, row_index):
    rows, width = table_ref.shape[1:]
    parts = width // BLOCK
    lines = jnp.concatenate(
        [table_ref[group, :, BLOCK * part : BLOCK * (part + 1)] for part in range(parts)], axis=0
    )
    results = []
    for piece in cells:
        cell = piece.astype(jnp.int32)
        lanes = cell.shape[1]
        chosen = jnp.where(
            lane_index[:, :lanes] == small_float(cell & (BLOCK - 1)), jnp.ones((), BF16), jnp.zeros((), BF16)
        )
        found = jnp.dot(lines, chosen, preferred_element_type=F32)
        part_of = cell >> 14
        kept = found[0:rows]
        for part in range(1, parts):
            kept = jnp.where(part_of == part, found[rows * part : rows * (part + 1)], kept)
        row_of = (cell >> 8) & (ROW_STRIDE - 1)
        value = jnp.sum(
            jnp.where(row_index[:, :lanes] == row_of, kept, 0.0), axis=0, keepdims=True
        )
        for half in range(lanes // LANES):
            results.append(value[:, LANES * half : LANES * (half + 1)])
    return results


def look_up_indices(rows):
    lane_index = small_float(lax.broadcasted_iota(jnp.int32, (BLOCK, BLOCK), 0))
    row_index = lax.broadcasted_iota(jnp.int32, (rows, BLOCK), 0)
    return lane_index, row_index


def pack_kernel(
    scalar_ref, level_ref, cell_ref, weight_ref, innov_ref, table_ref, send_out, target_ref, plane_ref, total_ref
):
    levels, rows, width = table_ref.shape
    lines = level_ref.shape[0]
    places = levels * RUN // BLOCK
    count = scalar_ref[0]
    first_rank = scalar_ref[1] * RUN
    slot = lax.broadcasted_iota(jnp.int32, (lines, LANES), 0) * LANES + lax.broadcasted_iota(
        jnp.int32, (lines, LANES), 1
    )
    level = jnp.where(slot < count, level_ref[...], levels)
    row_at = lax.broadcasted_iota(jnp.int32, (LANES, LANES), 0)
    lane_at = lax.broadcasted_iota(jnp.int32, (LANES, LANES), 1)
    upper = jnp.where(row_at <= lane_at, 1.0, 0.0).astype(BF16)
    ones = jnp.ones((LANES, LANES), BF16)
    before = jnp.where(
        lax.broadcasted_iota(jnp.int32, (lines, lines), 1)
        < lax.broadcasted_iota(jnp.int32, (lines, lines), 0),
        1.0,
        0.0,
    ).astype(BF16)
    rank = jnp.zeros((lines, LANES), F32)
    longest = jnp.zeros((1, LANES), F32)
    for index in range(levels):
        mask = level == index
        flags = jnp.where(mask, 1.0, 0.0).astype(BF16)
        inside = jnp.dot(flags, upper, preferred_element_type=F32)
        line_total = jnp.dot(flags, ones, preferred_element_type=F32)
        ahead = jnp.dot(before, line_total.astype(BF16), preferred_element_type=F32)
        rank = jnp.where(mask, ahead + inside - 1.0, rank)
        longest = jnp.maximum(longest, ahead[lines - 1 :, :] + line_total[lines - 1 :, :])
    place = rank.astype(jnp.int32) - first_rank
    kept = (level < levels) & (place >= 0) & (place < RUN)
    target_ref[...] = jnp.where(kept, level * RUN + place, -1)
    cell = cell_ref[...]
    plane_ref[0] = (cell & (BLOCK - 1)).astype(F32)
    plane_ref[1] = ((cell >> 8) - BLOCK // 2).astype(F32)
    for index, part in enumerate(split_three(weight_ref[...])):
        plane_ref[2 + index] = part
    for index, part in enumerate(split_three(innov_ref[...])):
        plane_ref[5 + index] = part
    total_ref[...] = jnp.zeros_like(total_ref)
    block_at = lax.broadcasted_iota(jnp.int32, (places, BLOCK), 0)
    lane_iota = lax.broadcasted_iota(jnp.int32, (BLOCK, BLOCK), 0)

    def pair_of(ref, index):
        return jnp.concatenate([ref[pl.ds(2 * index, 1), :], ref[pl.ds(2 * index + 1, 1), :]], axis=1)

    def place_block(index, carry):
        target = pair_of(target_ref, index)
        target_block = block_at == (target >> 8)
        target_lane = jnp.where(lane_iota == (target & (BLOCK - 1)), 1.0, 0.0).astype(BF16)
        parts = [
            jnp.where(target_block, pair_of(plane_ref.at[plane], index), 0.0).astype(BF16)
            for plane in range(PLANES)
        ]
        total_ref[...] += lax.dot_general(
            jnp.concatenate(parts, axis=0),
            target_lane,
            (((1,), (1,)), ((), ())),
            preferred_element_type=F32,
        )
        return carry

    lax.fori_loop(0, lines // 2, place_block, 0)
    planes = [total_ref[places * plane : places * (plane + 1), :] for plane in range(PLANES)]
    cell_sorted = (planes[1] + float(BLOCK // 2)) * float(BLOCK) + planes[0]
    weight_sorted = planes[2] + planes[3] + planes[4]
    innov_sorted = planes[5] + planes[6] + planes[7]
    for index in range(levels):
        for row in range(RUN_ROWS):
            line, half = divmod(index * RUN_ROWS + row, BLOCK // LANES)
            for plane, piece in enumerate((cell_sorted, weight_sorted, innov_sorted)):
                at = plane * RUN_ROWS + row
                send_out[index, at : at + 1, :] = piece[
                    line : line + 1, LANES * half : LANES * (half + 1)
                ]
        send_out[index, 4 * RUN_ROWS : SEND_ROWS, :] = jnp.broadcast_to(
            longest, (SEND_ROWS - 4 * RUN_ROWS, LANES)
        )
    lane_index, row_index = look_up_indices(rows)

    def one_level(index, carry):
        found = look_up(table_ref, index, run_pieces(send_out, index, 0), lane_index, row_index)
        for row in range(RUN_ROWS):
            at = 3 * RUN_ROWS + row
            send_out[index, at : at + 1, :] = found[row]
        return carry

    lax.fori_loop(0, levels, one_level, 0, unroll=UNROLL)


def pack_slots(scalars, level, cell, weight, innov, table):
    lines = level.shape[0]
    levels = table.shape[0]
    places = levels * RUN // BLOCK
    whole = pl.BlockSpec(memory_space=VMEM)
    return pl.pallas_call(
        pack_kernel,
        out_shape=jax.ShapeDtypeStruct((levels, SEND_ROWS, LANES), F32),
        in_specs=[pl.BlockSpec(memory_space=SMEM)] + [whole] * 5,
        out_specs=whole,
        scratch_shapes=[
            VMEM((lines, LANES), jnp.int32),
            VMEM((PLANES, lines, LANES), F32),
            VMEM((PLANES * places, BLOCK), F32),
        ],
        compiler_params=pltpu.CompilerParams(vmem_limit_bytes=16 << 20),
        cost_estimate=pl.CostEstimate(flops=25 * 10**9, bytes_accessed=4 << 20, transcendentals=0),
        name="pack_slots",
    )(scalars, level, cell, weight, innov, table)


def term_kernel(table_ref, run_ref, term_out):
    groups, rows, width = table_ref.shape
    lane_index, row_index = look_up_indices(rows)

    def one_group(group, carry):
        found = look_up(table_ref, group, run_pieces(run_ref, group, 0), lane_index, row_index)
        for row in range(RUN_ROWS):
            at = 3 * RUN_ROWS + row
            term_out[pl.ds(group * RUN_ROWS + row, 1), :] = (
                found[row] * run_ref[group, at : at + 1, :]
            )
        return carry

    lax.fori_loop(0, groups, one_group, 0, unroll=SLAB_UNROLL)


def slot_terms(table, runs):
    groups = table.shape[0]
    whole = pl.BlockSpec(memory_space=VMEM)
    return pl.pallas_call(
        term_kernel,
        out_shape=jax.ShapeDtypeStruct((groups * RUN_ROWS, LANES), F32),
        in_specs=[whole, whole],
        out_specs=whole,
        compiler_params=pltpu.CompilerParams(vmem_limit_bytes=12 << 20),
        cost_estimate=pl.CostEstimate(flops=4 * 10**9, bytes_accessed=3 << 20, transcendentals=0),
        name="slot_terms",
    )(table, runs)


def add_kernel(run_ref, model_ref, field_out):
    groups, rows, width = field_out.shape
    parts = width // BLOCK
    middle = ROW_STRIDE * parts // 2
    lane_index = small_float(lax.broadcasted_iota(jnp.int32, (BLOCK, RUN), 0))
    row_index = lax.broadcasted_iota(jnp.int32, (rows, RUN), 0)
    line_index = jnp.concatenate(
        [small_float(row_index + (ROW_STRIDE * part - middle)) for part in range(parts)], axis=0
    )

    def one_group(group, carry):
        def values_of(first):
            return jnp.concatenate(
                [run_ref[group, first + row : first + row + 1, :] for row in range(RUN_ROWS)], axis=1
            )

        cell = values_of(0).astype(jnp.int32)
        model = jnp.concatenate(
            [model_ref[pl.ds(group * RUN_ROWS + row, 1), :] for row in range(RUN_ROWS)], axis=1
        )
        weighted = values_of(RUN_ROWS) * (model - values_of(2 * RUN_ROWS))
        value = (values_of(3 * RUN_ROWS) * weighted).astype(BF16)
        lines = jnp.where(line_index == small_float((cell >> 8) - middle), value, jnp.zeros((), BF16))
        chosen = jnp.where(lane_index == small_float(cell & (BLOCK - 1)), jnp.ones((), BF16), jnp.zeros((), BF16))
        total = lax.dot_general(
            lines, chosen, (((1,), (1,)), ((), ())), preferred_element_type=F32
        )
        for part in range(parts):
            field_out[group, :, BLOCK * part : BLOCK * (part + 1)] = total[
                rows * part : rows * (part + 1), :
            ].astype(field_out.dtype)
        return carry

    lax.fori_loop(0, groups, one_group, 0, unroll=SLAB_UNROLL)


def add_slots(runs, model, rows, width, dtype):
    groups = runs.shape[0]
    whole = pl.BlockSpec(memory_space=VMEM)
    return pl.pallas_call(
        add_kernel,
        out_shape=jax.ShapeDtypeStruct((groups, rows, width), dtype),
        in_specs=[whole, whole],
        out_specs=whole,
        compiler_params=pltpu.CompilerParams(vmem_limit_bytes=16 << 20),
        cost_estimate=pl.CostEstimate(flops=4 * 10**9, bytes_accessed=3 << 20, transcendentals=0),
        name="add_slots",
    )(runs, model)


def localize(values, lat_root, lon_root):
    zonal = jnp.dot(values, lon_root, preferred_element_type=F32).astype(BF16)
    return jnp.dot(lat_root, zonal, preferred_element_type=F32)


def sum_members(value):
    members = lax.axis_size("mem")
    steps = [1 << bit for bit in range(members.bit_length() - 1)]
    for step in steps[:1] + steps[:0:-1]:
        value = value + lax.ppermute(value, "mem", [(i, i ^ step) for i in range(members)])
    return value


def exchange(value):
    return lax.all_to_all(value, "tile", split_axis=0, concat_axis=0, tiled=True)


def shards(
    alpha,
    perturbation,
    lon_scale,
    lat_scale,
    obs_level,
    obs_row,
    obs_col,
    obs_count,
    innovation,
    obs_weight,
):
    levels, rows, columns = alpha.shape[1:]
    tiles = lax.axis_size("tile")
    level = lax.axis_index("tile")
    slots = obs_level.shape[1]
    pad_rows = round_up(rows, 16)
    width = round_up(columns, BLOCK)
    padding = ((0, 0), (0, pad_rows - rows), (0, width - columns))

    alpha_slab = exchange(jnp.pad(alpha[0], padding))

    as_lines = lambda value: value.reshape(slots // LANES, LANES)
    column = as_lines(obs_col)
    cell = ((column >> 8) * ROW_STRIDE + as_lines(obs_row)) * BLOCK + (column & (BLOCK - 1))
    pert_table = jnp.pad(perturbation[0], padding)

    def packed_chunk(chunk):
        scalars = jnp.stack([obs_count[0], chunk])
        return pack_slots(
            scalars,
            as_lines(obs_level),
            cell,
            as_lines(obs_weight),
            as_lines(innovation),
            pert_table,
        )

    alpha_slab, packed = lax.optimization_barrier((alpha_slab, packed_chunk(jnp.int32(0))))
    runs = exchange(packed)
    longest = jnp.max(runs[:, SEND_ROWS - 1, 0]).astype(jnp.int32)

    column_at = jnp.arange(width)
    lon_root = square_root(
        lax.dynamic_index_in_dim(lon_scale, level, keepdims=False),
        column_at,
        column_at < columns,
        columns,
        True,
    )
    line = jnp.arange(tiles * pad_rows)
    row_in_band = line % pad_rows
    lat_root = square_root(
        lax.dynamic_index_in_dim(lat_scale, level, keepdims=False),
        (line // pad_rows) * rows + row_in_band,
        row_in_band < rows,
        rows * tiles,
        False,
    )
    lon_root, lat_root = lax.optimization_barrier((lon_root, lat_root))

    padded = alpha_slab.reshape(tiles * pad_rows, width)
    spread = localize(padded, lat_root, lon_root).astype(BF16).reshape(tiles, pad_rows, width)

    def chunk_field(chunk_run, dtype):
        model = sum_members(slot_terms(spread, chunk_run))
        return add_slots(chunk_run, model, pad_rows, width, dtype)

    def gradient_of(field):
        back = localize(field.reshape(tiles * pad_rows, width), lat_root, lon_root)
        return (padded.astype(F32) + back).astype(BF16).reshape(tiles, pad_rows, width)

    def many_runs(_):
        def one_chunk(chunk, field):
            return field + chunk_field(exchange(packed_chunk(chunk)), F32)

        start = jnp.zeros((tiles, pad_rows, width), F32)
        chunks = (longest + RUN - 1) // RUN
        return gradient_of(lax.fori_loop(0, chunks, one_chunk, start).astype(BF16))

    first = lax.optimization_barrier(gradient_of(chunk_field(runs, BF16)))
    gradient = lax.cond(longest > RUN, many_runs, lambda done: done, first)
    return exchange(gradient)[None, :, :rows, :columns]


def solution(mesh):
    in_specs = (
        P("mem", None, "tile", None),
        P("mem", None, "tile", None),
        P(),
        P(),
        P("tile", None),
        P("tile", None),
        P("tile", None),
        P("tile"),
        P("tile", None),
        P("tile", None),
    )
    out_specs = P("mem", None, "tile", None)
    return jax.shard_map(shards, mesh=mesh, in_specs=in_specs, out_specs=out_specs, check_vma=False)
```
